256 devices in a mesh: blk: 128 (over y_lo, x, z, core), pair: 2 (over y_hi).
Axes of the slice: x: 4, y: 4 (y_hi: 2, y_lo: 2; y = y_hi * 2 + y_lo), z: 8, core: 2. Of those that a mesh axis runs over, the one named last changes fastest.
Arguments:
- vertex: bfloat16 [128, 2048, 2048], P('blk', 'pair'), may hold values from -0.125 to 0.125
- left_phase: bfloat16 [128, 2048, 512], P('blk', 'pair'), may hold values from -6 to 6
- right_phase: bfloat16 [128, 2048, 512], P('blk'), may hold values from -6 to 6
- tiles: bfloat16 [512, 512, 512], P('blk'), may hold values from -0.25 to 0.25
- orders: int32 [128], P('blk'), may hold values from 512 to 2048, as said below
- momentum: int32 [512], replicated, may hold values from 0 to 63
- frequency: int32 [512], replicated, may hold values from 0 to 31
Outputs:
- suscept: bfloat16 [512, 512, 512], P('blk', 'pair')
- sigma: float32 [2048], P(('blk', 'pair'))
The draws below stay inside these ranges and needn't reach their ends.
Inputs may be any that keep to these rules, and one draw needn't show every extreme that they name: `orders`: every order is at least 512 and at most 2048; some walker has order exactly 2048.
All inputs are finite; a program needn't handle non-finite values.
Results may differ from the reference program's by a relative error of at most 0.0075.
Values may be sent and summed in bfloat16 or wider, within the bound.
No kernel may reach another device: no remote copies, remote signals or barrier semaphores. Data moves between devices by JAX's collectives and lax.ppermute only.
A program may use at most 64 MiB of HBM per device.

```python
import math
import jax
import jax.numpy as jnp
from jax import lax

S = 512
KMAX = 2048
TILES_DEV = 4
NMOM = 64
NFREQ = 32
WALKERS = 128
TILES = 512
N_BLK = 128


def draw_orders(key, part):
    values = jax.random.randint(key, (WALKERS,), KMAX // 4, KMAX + 1)
    chosen = jax.random.randint(jax.random.fold_in(key, 7), (), 0, WALKERS)
    return values.at[chosen].set(KMAX).astype(jnp.int32)


def touch_ends(array, stream_key, smallest, largest):
    longest = array.shape.index(max(array.shape))
    spots = []
    for shift in (0, 1):
        where = [jax.random.randint(jax.random.fold_in(stream_key, axis), (), 0, length) for axis, length in enumerate(array.shape)]
        where[longest] = (where[longest] + shift) % array.shape[longest]
        spots.append(tuple(where))
    return array.at[spots[0]].set(smallest).at[spots[1]].set(largest)


def block_scale(own_key, extent, split, low, largest):
    def one(position, shards_of):
        heights = jax.random.uniform(jax.random.fold_in(jax.random.fold_in(own_key, 6), position), (shards_of,), jnp.float32, low / len(split), largest / len(split))
        return jnp.repeat(jnp.exp(heights), extent[position] // shards_of).reshape((-1,) + (1,) * (len(extent) - position - 1))

    loudness = one(*split[0])
    for cut in split[1:]:
        loudness = loudness * one(*cut)
    return loudness


def normal_values(rng, extent, width, limit, split=(), kind=jnp.bfloat16):
    gain = block_scale(rng, extent, split, -0.22, 0.18) if split else 1.0
    values = jax.random.normal(rng, extent, jnp.float32) * width * gain
    return jnp.minimum(jnp.maximum(values, -limit), limit).astype(kind)


def setup_inputs(seed: int = 0) -> dict:
    seeds = jax.random.split(jax.random.key(seed), 8)
    return {
        "vertex": normal_values(seeds[0], (WALKERS, KMAX, KMAX), KMAX ** -0.5, 0.125, ((0, 128), (1, 2))),
        "left_phase": normal_values(seeds[1], (WALKERS, KMAX, S), 1.0, 6.0, ((0, 128), (1, 2))),
        "right_phase": normal_values(seeds[2], (WALKERS, KMAX, S), 1.0, 6.0, ((0, 128),)),
        "tiles": normal_values(seeds[3], (TILES, S, S), S ** -0.5, 0.25, ((0, 128),)),
        "orders": draw_orders(jax.random.fold_in(seeds[7], 71), 0),
        "momentum": touch_ends(jax.random.randint(seeds[5], (S,), 0, NMOM), jax.random.fold_in(seeds[5], 1), 0, NMOM - 1).astype(jnp.int32),
        "frequency": touch_ends(jax.random.randint(seeds[6], (S,), 0, NFREQ), jax.random.fold_in(seeds[6], 1), 0, NFREQ - 1).astype(jnp.int32),
    }


def reference(vertex, left_phase, right_phase, tiles, orders, momentum, frequency):
    positions = jnp.arange(KMAX, dtype=jnp.int32)

    def one_walker(items):
        matrix, left, right, order = items
        live = positions < order
        masked = jnp.where(live[:, None] & live[None, :], matrix, jnp.zeros_like(matrix))
        carried = jnp.dot(masked, right, preferred_element_type=jnp.float32).astype(jnp.bfloat16)
        green = lax.dot_general(left, carried, (((0,), (0,)), ((), ())), preferred_element_type=jnp.float32)
        return (green / math.sqrt(KMAX)).astype(jnp.bfloat16)
    greens = lax.map(one_walker, (vertex, left_phase, right_phase, orders))
    grouped = tiles.reshape(N_BLK, TILES_DEV, S, S)
    onehot_mom = (momentum[:, None] == jnp.arange(NMOM, dtype=jnp.int32)[None, :]).astype(jnp.float32)
    onehot_freq = (frequency[:, None] == jnp.arange(NFREQ, dtype=jnp.int32)[None, :]).astype(jnp.float32)
    offsets = jnp.arange(-2, 3, dtype=jnp.int32)

    def one_block(number):
        window = jnp.take(greens, (number + offsets) % N_BLK, axis=0).astype(jnp.float32)
        block_tiles = grouped[number].astype(jnp.float32)
        inner = jnp.einsum('usa,tab->utsb', window, block_tiles).astype(jnp.bfloat16).astype(jnp.float32)
        chi = jnp.einsum('utsb,ucb->tsc', inner, window) / math.sqrt(S)
        summed = lax.optimization_barrier(jnp.sum(chi, axis=0))
        partial_value = jnp.dot(summed, onehot_freq, precision=lax.Precision.HIGHEST)
        cells = jnp.dot(onehot_mom.T, partial_value, precision=lax.Precision.HIGHEST)
        return (chi.astype(jnp.bfloat16), cells)
    chis, cells = lax.map(one_block, jnp.arange(N_BLK, dtype=jnp.int32))
    factor = 1.0 / math.sqrt(5.0 * TILES_DEV * N_BLK * S * S / (NMOM * NFREQ))
    sigma = (lax.optimization_barrier(jnp.sum(cells, axis=0)) * factor).reshape(-1)
    return (chis.reshape(TILES_DEV * N_BLK, S, S), sigma)
```

```python
import functools
import math

import jax
import jax.numpy as jnp
from jax import lax
from jax.experimental import pallas as pl
from jax.experimental.pallas import tpu as pltpu
from jax.sharding import PartitionSpec as P

NMOM = 64
NFREQ = 32
BOTH = ("blk", "pair")
F32 = jnp.float32
BF16 = jnp.bfloat16
CHUNKS = 4
MIB = 1024 * 1024


def split_dot(left, right, dims):
    def halves(value):
        high = value.astype(BF16)
        return high, (value - high.astype(F32)).astype(BF16)

    (a_high, a_low), (b_high, b_low) = halves(left), halves(right)
    dot = functools.partial(lax.dot_general, dimension_numbers=(dims, ((), ())), preferred_element_type=F32)
    return dot(a_high, b_high) + dot(a_high, b_low) + dot(a_low, b_high)


def partial_kernel(
    scale, order_ref, vertex_hbm, right_hbm, left_hbm, exact_ref, sent_ref,
    vertex, right, left, total, sems,
):
    order = order_ref[0]
    first_row = lax.axis_index("pair") * total.shape[0]
    depth, states = right.shape[1:]
    copies = []
    for k in range(CHUNKS):
        span = pl.ds(k * depth, depth)
        copies.append(
            (
                pltpu.make_async_copy(right_hbm.at[span, :], right.at[k], sems.at[2 * k]),
                pltpu.make_async_copy(vertex_hbm.at[:, span], vertex.at[k], sems.at[2 * k + 1]),
            )
        )
    left_copy = pltpu.make_async_copy(left_hbm, left, sems.at[2 * CHUNKS])
    for pieces in copies:
        for copy in pieces:
            copy.start()
    left_copy.start()
    for k, pieces in enumerate(copies):
        for copy in pieces:
            copy.wait()

        @pl.when(order < (k + 1) * depth)
        def _():
            rows = lax.broadcasted_iota(jnp.int32, (depth, states), 0)
            right[k] = jnp.where(rows < order - k * depth, right[k], jnp.zeros_like(right[k]))

        product = jnp.dot(vertex[k], right[k], preferred_element_type=F32)
        if k == 0:
            total[...] = product
        else:
            total[...] += product
    left_copy.wait()
    live = lax.broadcasted_iota(jnp.int32, total.shape, 0) < order - first_row
    carried = jnp.where(live, total[...], 0.0).astype(BF16)
    green = (
        lax.dot_general(
            left[...], carried, (((0,), (0,)), ((), ())), preferred_element_type=F32
        )
        * scale
    )
    exact_ref[...] = green
    sent_ref[...] = green.astype(BF16)


def partial_green(order, vertex, right, left):
    height, breadth = vertex.shape
    states = right.shape[1]
    depth = breadth // CHUNKS
    hbm = pl.BlockSpec(memory_space=pltpu.HBM)
    vmem = pl.BlockSpec(memory_space=pltpu.VMEM)
    return pl.pallas_call(
        functools.partial(partial_kernel, 1.0 / math.sqrt(breadth)),
        in_specs=[pl.BlockSpec(memory_space=pltpu.SMEM), hbm, hbm, hbm],
        out_specs=[vmem] * 2,
        out_shape=[
            jax.ShapeDtypeStruct((states, states), F32),
            jax.ShapeDtypeStruct((states, states), BF16),
        ],
        scratch_shapes=[
            pltpu.VMEM((CHUNKS, height, depth), BF16),
            pltpu.VMEM((CHUNKS, depth, states), BF16),
            pltpu.VMEM((height, states), BF16),
            pltpu.VMEM((height, states), F32),
            pltpu.SemaphoreType.DMA((2 * CHUNKS + 1,)),
        ],
        compiler_params=pltpu.CompilerParams(vmem_limit_bytes=60 * MIB),
        cost_estimate=pl.CostEstimate(
            flops=2 * height * states * (breadth + states),
            bytes_accessed=2 * (height * breadth + breadth * states + height * states),
            transcendentals=0,
        ),
        name="partial_green",
    )(order, vertex, right, left)


def green_kernel(exact_ref, got_ref, green_ref):
    green_ref[...] = (exact_ref[...] + got_ref[...].astype(F32)).astype(BF16)


def whole_green(exact, got):
    vmem = pl.BlockSpec(memory_space=pltpu.VMEM)
    return pl.pallas_call(
        green_kernel,
        in_specs=[vmem] * 2,
        out_specs=vmem,
        out_shape=jax.ShapeDtypeStruct(exact.shape, BF16),
        compiler_params=pltpu.CompilerParams(vmem_limit_bytes=16 * MIB),
        cost_estimate=pl.CostEstimate(
            flops=exact.size, bytes_accessed=8 * exact.size, transcendentals=0
        ),
        name="whole_green",
    )(exact, got)


def sigma_kernel(factor, walkers, sum_ref, mom_ref, freq_ref, *refs):
    greens, (out_ref, stacked, left, right) = refs[:walkers], refs[walkers:]
    half, states = sum_ref.shape
    pick_mom = (lax.broadcasted_iota(jnp.int32, (NMOM, states), 0) == mom_ref[...]).astype(BF16)
    pick_freq = (lax.broadcasted_iota(jnp.int32, (NFREQ, states), 0) == freq_ref[...]).astype(BF16)
    first = pl.multiple_of(lax.axis_index("pair") * half, half)
    for u, ref in enumerate(greens):
        stacked[u * NMOM : (u + 1) * NMOM, :] = jnp.dot(
            pick_mom, ref[:, pl.ds(first, half)], preferred_element_type=F32
        )
        right[:, u * states : (u + 1) * states] = jnp.dot(
            pick_freq, ref[...], preferred_element_type=F32
        )
    folded = split_dot(stacked[...], sum_ref[...], ((1,), (0,)))
    for u in range(walkers):
        left[:, u * states : (u + 1) * states] = folded[u * NMOM : (u + 1) * NMOM]
    cells = split_dot(left[...], right[...], ((1,), (1,)))
    owners, width = out_ref.shape
    fold = NFREQ // width
    owner = lax.broadcasted_iota(jnp.int32, (owners, NMOM), 0)
    column = lax.broadcasted_iota(jnp.int32, (owners, NMOM), 1)
    spread = jnp.dot(
        (owner // fold == column).astype(F32),
        cells * factor,
        precision=lax.Precision.HIGHEST,
        preferred_element_type=F32,
    )
    turn = lax.broadcasted_iota(jnp.int32, (owners, width), 0) % fold
    result = jnp.zeros((owners, width), F32)
    for part in range(fold):
        result = jnp.where(turn == part, spread[:, part * width : (part + 1) * width], result)
    out_ref[...] = result


def sigma_cells(factor, tile_sum, greens, momentum, frequency, owners):
    width = NMOM * NFREQ // owners
    states = tile_sum.shape[1]
    vmem = pl.BlockSpec(memory_space=pltpu.VMEM)
    return pl.pallas_call(
        functools.partial(sigma_kernel, factor, len(greens)),
        in_specs=[vmem] * (3 + len(greens)),
        out_specs=vmem,
        out_shape=jax.ShapeDtypeStruct((owners, width), F32),
        scratch_shapes=[
            pltpu.VMEM((len(greens) * NMOM, states // 2), F32),
            pltpu.VMEM((NMOM, len(greens) * states), F32),
            pltpu.VMEM((NFREQ, len(greens) * states), F32),
        ],
        compiler_params=pltpu.CompilerParams(vmem_limit_bytes=16 * MIB),
        cost_estimate=pl.CostEstimate(flops=400_000_000, bytes_accessed=1_600_000, transcendentals=0),
        name="sigma_cells",
    )(tile_sum, momentum[None, :], frequency[None, :], *greens)


def chi_kernel(walkers, scale, *refs):
    greens, tile_ref, rest = refs[:walkers], refs[walkers], refs[walkers + 1 :]
    out_ref = rest[-1]
    half = out_ref.shape[1]
    first = pl.multiple_of(lax.axis_index("pair") * half, half)
    tile = tile_ref[0]
    total = None if len(rest) == 1 else rest[0][0]
    for green in greens:
        upper = green[pl.ds(first, half), :]
        inner = jnp.dot(upper, tile, preferred_element_type=F32).astype(BF16)
        term = lax.dot_general(
            inner, green[...], (((1,), (1,)), ((), ())), preferred_element_type=F32
        )
        total = term if total is None else total + term
    out_ref[0] = (total * scale).astype(out_ref.dtype)


def chi_terms(greens, tiles, running, scale, dtype, limit):
    count, states, _ = tiles.shape
    half = states // 2
    extra = [] if running is None else [running]
    whole = pl.BlockSpec((states, states), lambda t: (0, 0))
    rows = pl.BlockSpec((1, half, states), lambda t: (t, 0, 0))
    return pl.pallas_call(
        functools.partial(chi_kernel, len(greens), scale),
        grid=(count,),
        in_specs=[whole] * len(greens)
        + [pl.BlockSpec((1, states, states), lambda t: (t, 0, 0))]
        + [rows] * len(extra),
        out_specs=rows,
        out_shape=jax.ShapeDtypeStruct((count, half, states), dtype),
        compiler_params=pltpu.CompilerParams(vmem_limit_bytes=limit * MIB),
        cost_estimate=pl.CostEstimate(
            flops=len(greens) * count * 4 * half * states * states,
            bytes_accessed=2 * states * states * (count + len(greens)) + 4 * count * half * states,
            transcendentals=0,
        ),
        name="chi_terms",
    )(*greens, tiles, *extra)


def moves(mesh_shape):
    blk, pair = mesh_shape

    def flat(rule):
        return [(b * pair + p, rule(b, p)) for b in range(blk) for p in range(pair)]

    other = flat(lambda b, p: b * pair + (p + 1) % pair)
    core = flat(lambda b, p: (b ^ 1) * pair + p)

    def along(even, odd):
        return flat(lambda b, p: ((b + (odd if b % 2 else even)) % blk) * pair + p)

    return other, core, along(2, -2), along(-2, 2)


def send(value, pairs):
    return lax.ppermute(value, BOTH, pairs)


def per_device(vertex, left_phase, right_phase, tiles, orders, momentum, frequency):
    states = right_phase.shape[2]
    half = states // 2
    blk, pair = lax.axis_size("blk"), lax.axis_size("pair")
    other, core, outward, inward = moves((blk, pair))

    with jax.named_scope("green"):
        exact, sent = partial_green(orders, vertex[0], right_phase[0], left_phase[0])
        received = send(sent, other)
        own_rows = lax.dynamic_slice_in_dim(tiles, lax.axis_index("pair") * half, half, 1)
        tile_sum = jnp.sum(own_rows.astype(F32), axis=0)
        received, tile_sum = lax.optimization_barrier((received, tile_sum))
        green = whole_green(exact, received)

    with jax.named_scope("window"):
        green_core = send(green, core)
        green_in = send(green, inward)
        green_out = send(green, outward)
        running = chi_terms([green, green_core], tiles, None, 1.0, F32, 24)
        running, green_in = lax.optimization_barrier((running, green_in))
        green_last = send(green_in, core)
        far = [green_in, green_out, green_last]

    with jax.named_scope("sigma"):
        factor = 1.0 / math.sqrt(
            5.0 * tiles.shape[0] * blk * states * states / (NMOM * NFREQ)
        ) / math.sqrt(states)
        cells = sigma_cells(
            factor, tile_sum, [green, green_core] + far, momentum, frequency, blk * pair
        )
        running, cells = lax.optimization_barrier((running, cells))
        spread = lax.all_to_all(cells, BOTH, 0, 0, tiled=True)

    with jax.named_scope("chi"):
        suscept = chi_terms(far, tiles, running, 1.0 / math.sqrt(states), BF16, 60)
        suscept, spread = lax.optimization_barrier((suscept, spread))
        owned = jnp.sum(spread, axis=0)
    return suscept, owned


def solution(mesh):
    in_specs = (
        P("blk", "pair", None),
        P("blk", "pair", None),
        P("blk", None, None),
        P("blk", None, None),
        P("blk"),
        P(),
        P(),
    )
    out_specs = (P("blk", "pair", None), P(("blk", "pair")))
    return jax.shard_map(
        per_device, mesh=mesh, in_specs=in_specs, out_specs=out_specs, check_vma=False
    )
```

```python
import functools
import math

import jax
import jax.numpy as jnp
from jax import lax
from jax.experimental import pallas as pl
from jax.experimental.pallas import tpu as pltpu
from jax.sharding import PartitionSpec as P

NMOM = 64
NFREQ = 32
BOTH = ("blk", "pair")
F32 = jnp.float32
BF16 = jnp.bfloat16
CHUNKS = 4
MIB = 1024 * 1024


def split_rows(value):
    high = value.astype(BF16)
    return jnp.concatenate([high, (value - high.astype(F32)).astype(BF16)], axis=0)


def across(left, right):
    return lax.dot_general(left, right, (((1,), (1,)), ((), ())), preferred_element_type=F32)


def partial_kernel(
    scale, order_ref, vertex_hbm, right_hbm, left_hbm, exact_ref, sent_ref,
    vertex, right, left, total, sems,
):
    order = order_ref[0]
    first_row = lax.axis_index("pair") * total.shape[0]
    depth, states = right.shape[1:]
    copies = []
    for k in range(CHUNKS):
        span = pl.ds(k * depth, depth)
        copies.append(
            (
                pltpu.make_async_copy(right_hbm.at[span, :], right.at[k], sems.at[2 * k]),
                pltpu.make_async_copy(vertex_hbm.at[:, span], vertex.at[k], sems.at[2 * k + 1]),
            )
        )
    left_copy = pltpu.make_async_copy(left_hbm, left, sems.at[2 * CHUNKS])
    for pieces in copies:
        for copy in pieces:
            copy.start()
    left_copy.start()
    for k, pieces in enumerate(copies):
        for copy in pieces:
            copy.wait()

        @pl.when(order < (k + 1) * depth)
        def _():
            rows = lax.broadcasted_iota(jnp.int32, (depth, states), 0)
            right[k] = jnp.where(rows < order - k * depth, right[k], jnp.zeros_like(right[k]))

        product = jnp.dot(vertex[k], right[k], preferred_element_type=F32)
        if k == 0:
            total[...] = product
        else:
            total[...] += product
    left_copy.wait()
    live = lax.broadcasted_iota(jnp.int32, total.shape, 0) < order - first_row
    carried = jnp.where(live, total[...], 0.0).astype(BF16)
    green = (
        lax.dot_general(
            left[...], carried, (((0,), (0,)), ((), ())), preferred_element_type=F32
        )
        * scale
    )
    exact_ref[...] = green
    sent_ref[...] = green.astype(BF16)


def partial_green(order, vertex, right, left):
    height, breadth = vertex.shape
    states = right.shape[1]
    depth = breadth // CHUNKS
    hbm = pl.BlockSpec(memory_space=pltpu.HBM)
    vmem = pl.BlockSpec(memory_space=pltpu.VMEM)
    return pl.pallas_call(
        functools.partial(partial_kernel, 1.0 / math.sqrt(breadth)),
        in_specs=[pl.BlockSpec(memory_space=pltpu.SMEM), hbm, hbm, hbm],
        out_specs=[vmem] * 2,
        out_shape=[
            jax.ShapeDtypeStruct((states, states), F32),
            jax.ShapeDtypeStruct((states, states), BF16),
        ],
        scratch_shapes=[
            pltpu.VMEM((CHUNKS, height, depth), BF16),
            pltpu.VMEM((CHUNKS, depth, states), BF16),
            pltpu.VMEM((height, states), BF16),
            pltpu.VMEM((height, states), F32),
            pltpu.SemaphoreType.DMA((2 * CHUNKS + 1,)),
        ],
        compiler_params=pltpu.CompilerParams(vmem_limit_bytes=24 * MIB),
        cost_estimate=pl.CostEstimate(
            flops=2 * height * states * (breadth + states),
            bytes_accessed=2 * (height * breadth + breadth * states + height * states),
            transcendentals=0,
        ),
        name="partial_green",
    )(order, *[pltpu.with_memory_space_constraint(x, pltpu.HBM) for x in (vertex, right, left)])


def green_kernel(exact_ref, got_ref, green_ref):
    green_ref[...] = (exact_ref[...] + got_ref[...].astype(F32)).astype(BF16)


def whole_green(exact, got):
    vmem = pl.BlockSpec(memory_space=pltpu.VMEM)
    return pl.pallas_call(
        green_kernel,
        in_specs=[vmem] * 2,
        out_specs=vmem,
        out_shape=jax.ShapeDtypeStruct(exact.shape, BF16),
        compiler_params=pltpu.CompilerParams(vmem_limit_bytes=16 * MIB),
        cost_estimate=pl.CostEstimate(
            flops=exact.size, bytes_accessed=8 * exact.size, transcendentals=0
        ),
        name="whole_green",
    )(exact, got)


def fold_walker(green, pick_mom, pick_freq, tile_sum):
    rows, width = pick_mom.shape[0], pick_freq.shape[0]
    by_mom = split_rows(jnp.dot(pick_mom, green, preferred_element_type=F32))
    both = jnp.dot(by_mom, tile_sum, preferred_element_type=F32)
    folded = split_rows(both[:rows] + both[rows:])
    by_freq = split_rows(jnp.dot(pick_freq, green, preferred_element_type=F32))
    terms = across(folded, by_freq)
    terms = terms[:rows] + terms[rows:]
    return terms[:, :width] + terms[:, width:]


def picks(mom_ref, freq_ref, rows, width):
    states = mom_ref.shape[1]
    per_row = rows // NMOM
    mom = lax.broadcasted_iota(jnp.int32, (rows, states), 0) // per_row == mom_ref[...]
    freq = lax.broadcasted_iota(jnp.int32, (width, states), 0) == freq_ref[...]
    return mom.astype(F32).astype(BF16), freq.astype(F32).astype(BF16)


def own_kernel(green_ref, sum_ref, mom_ref, freq_ref, out_ref):
    pick_mom, pick_freq = picks(mom_ref, freq_ref, *out_ref.shape)
    out_ref[...] = fold_walker(green_ref[...], pick_mom, pick_freq, sum_ref[...])


def sigma_kernel(factor, cells_ref, in_ref, far_ref, chip_ref, own_ref, mom_ref, freq_ref, out_ref):
    pick_mom, pick_freq = picks(mom_ref, freq_ref, *cells_ref.shape)
    cells = (
        cells_ref[...]
        + fold_walker(in_ref[...], pick_mom, pick_freq, chip_ref[...])
        + fold_walker(far_ref[...], pick_mom, pick_freq, own_ref[...])
    ) * factor
    rows, width = out_ref.shape
    owner = lax.broadcasted_iota(jnp.int32, (rows, width), 0) * lax.axis_size(
        "pair"
    ) + lax.axis_index("pair")
    fold = NFREQ // width
    result = jnp.zeros((rows, width), F32)
    for part in range(fold):
        result = jnp.where(
            owner % fold == part, cells[:, part * width : (part + 1) * width], result
        )
    out_ref[...] = result


def small_call(kernel, shape, flops, name):
    vmem = pl.BlockSpec(memory_space=pltpu.VMEM)

    def call(*operands):
        return pl.pallas_call(
            kernel,
            in_specs=[vmem] * len(operands),
            out_specs=vmem,
            out_shape=jax.ShapeDtypeStruct(shape, F32),
            compiler_params=pltpu.CompilerParams(vmem_limit_bytes=16 * MIB),
            cost_estimate=pl.CostEstimate(
                flops=flops, bytes_accessed=sum(2 * x.size for x in operands), transcendentals=0
            ),
            name=name,
        )(*operands)

    return call


def chi_kernel(walkers, scale, *refs):
    greens, tile_ref, rest = refs[:walkers], refs[walkers], refs[walkers + 1 :]
    out_ref = rest[-1]
    half = out_ref.shape[1]
    first = pl.multiple_of(lax.axis_index("pair") * half, half)
    tile = tile_ref[0]
    total = None if len(rest) == 1 else rest[0][0]
    for green in greens:
        upper = green[pl.ds(first, half), :]
        inner = jnp.dot(upper, tile, preferred_element_type=F32).astype(BF16)
        term = lax.dot_general(
            inner, green[...], (((1,), (1,)), ((), ())), preferred_element_type=F32
        )
        total = term if total is None else total + term
    out_ref[0] = (total * scale).astype(out_ref.dtype)


def chi_terms(greens, tiles, running, scale, dtype, limit):
    count, states, _ = tiles.shape
    half = states // 2
    extra = [] if running is None else [running]
    whole = pl.BlockSpec((states, states), lambda t: (0, 0))
    rows = pl.BlockSpec((1, half, states), lambda t: (t, 0, 0))
    return pl.pallas_call(
        functools.partial(chi_kernel, len(greens), scale),
        grid=(count,),
        in_specs=[whole] * len(greens)
        + [pl.BlockSpec((1, states, states), lambda t: (t, 0, 0))]
        + [rows] * len(extra),
        out_specs=rows,
        out_shape=jax.ShapeDtypeStruct((count, half, states), dtype),
        compiler_params=pltpu.CompilerParams(vmem_limit_bytes=limit * MIB),
        cost_estimate=pl.CostEstimate(
            flops=len(greens) * count * 4 * half * states * states,
            bytes_accessed=2 * states * states * (count + len(greens)) + 4 * count * half * states,
            transcendentals=0,
        ),
        name="chi_terms",
    )(*greens, tiles, *[pltpu.with_memory_space_constraint(x, pltpu.HBM) for x in extra])


def moves(mesh_shape):
    blk, pair = mesh_shape

    def flat(rule):
        return [(b * pair + p, rule(b, p)) for b in range(blk) for p in range(pair)]

    other = flat(lambda b, p: b * pair + (p + 1) % pair)
    core = flat(lambda b, p: (b ^ 1) * pair + p)

    def along(even, odd):
        return flat(lambda b, p: ((b + (odd if b % 2 else even)) % blk) * pair + p)

    return other, core, along(2, -2), along(-2, 2)


def send(value, pairs):
    return lax.ppermute(value, BOTH, pairs)


def per_device(vertex, left_phase, right_phase, tiles, orders, momentum, frequency):
    states = right_phase.shape[2]
    half = states // 2
    blk, pair = lax.axis_size("blk"), lax.axis_size("pair")
    other, core, outward, inward = moves((blk, pair))

    with jax.named_scope("green"):
        exact, sent = partial_green(orders, vertex[0], right_phase[0], left_phase[0])
        sent, later_tiles = lax.optimization_barrier((sent, tiles))
        received = send(sent, other)
        own_sum = jnp.sum(later_tiles.astype(F32), axis=0)
        sent_sum = own_sum.astype(BF16)
        chip_sum = (own_sum + send(sent_sum, core).astype(F32)).astype(BF16)
        received, sent_sum, chip_sum = lax.optimization_barrier((received, sent_sum, chip_sum))
        green = whole_green(exact, received)

    with jax.named_scope("window"):
        mom, freq = momentum[None, :], frequency[None, :]
        green_core = send(green, core)
        green_in = send(green, inward)
        green_out = send(green, outward)
        running = chi_terms([green, green_core], tiles, None, 1.0, F32, 24)
        cells = small_call(own_kernel, (blk, NFREQ), 200_000_000, "own_cells")(
            green, chip_sum, mom, freq
        )
        running, cells, green_in = lax.optimization_barrier((running, cells, green_in))
        green_last = send(green_in, core)

    with jax.named_scope("sigma"):
        factor = 1.0 / math.sqrt(
            5.0 * tiles.shape[0] * blk * states * states / (NMOM * NFREQ)
        ) / math.sqrt(states)
        cells = small_call(
            functools.partial(sigma_kernel, factor),
            (blk, NMOM * NFREQ // (blk * pair)),
            400_000_000,
            "sigma_cells",
        )(cells, green_in, green_out, chip_sum, sent_sum, mom, freq)
        running, cells = lax.optimization_barrier((running, cells))
        spread = lax.all_to_all(cells, "blk", 0, 0, tiled=True)

    with jax.named_scope("chi"):
        far = [green_in, green_out, green_last]
        suscept = chi_terms(far, tiles, running, 1.0 / math.sqrt(states), BF16, 24)
        suscept, spread = lax.optimization_barrier((suscept, spread))
        owned = jnp.sum(spread, axis=0)
    return suscept, owned


def solution(mesh):
    in_specs = (
        P("blk", "pair", None),
        P("blk", "pair", None),
        P("blk", None, None),
        P("blk", None, None),
        P("blk"),
        P(),
        P(),
    )
    out_specs = (P("blk", "pair", None), P(("blk", "pair")))
    return jax.shard_map(
        per_device, mesh=mesh, in_specs=in_specs, out_specs=out_specs, check_vma=False
    )
```

```python
import functools
import math

import jax
import jax.numpy as jnp
from jax import lax
from jax.experimental import pallas as pl
from jax.experimental.pallas import tpu as pltpu
from jax.sharding import PartitionSpec as P

NMOM = 64
NFREQ = 32
BOTH = ("blk", "pair")
F32 = jnp.float32
BF16 = jnp.bfloat16
CHUNKS = 4
MIB = 1024 * 1024


def split_rows(value):
    high = value.astype(BF16)
    return jnp.concatenate([high, (value - high.astype(F32)).astype(BF16)], axis=0)


def across(left, right):
    return lax.dot_general(left, right, (((1,), (1,)), ((), ())), preferred_element_type=F32)


def partial_kernel(
    scale, order_ref, vertex_hbm, right_hbm, left_hbm, exact_ref, sent_ref,
    vertex, right, left, total, sems,
):
    order = order_ref[0]
    first_row = lax.axis_index("pair") * total.shape[0]
    depth, states = right.shape[1:]
    copies = []
    for k in range(CHUNKS):
        span = pl.ds(k * depth, depth)
        copies.append(
            (
                pltpu.make_async_copy(right_hbm.at[span, :], right.at[k], sems.at[2 * k]),
                pltpu.make_async_copy(vertex_hbm.at[:, span], vertex.at[k], sems.at[2 * k + 1]),
            )
        )
    left_copy = pltpu.make_async_copy(left_hbm, left, sems.at[2 * CHUNKS])
    for pieces in copies:
        for copy in pieces:
            copy.start()
    left_copy.start()
    for k, pieces in enumerate(copies):
        for copy in pieces:
            copy.wait()

        @pl.when(order < (k + 1) * depth)
        def _():
            rows = lax.broadcasted_iota(jnp.int32, (depth, states), 0)
            right[k] = jnp.where(rows < order - k * depth, right[k], jnp.zeros_like(right[k]))

        product = jnp.dot(vertex[k], right[k], preferred_element_type=F32)
        if k == 0:
            total[...] = product
        else:
            total[...] += product
    left_copy.wait()
    live = lax.broadcasted_iota(jnp.int32, total.shape, 0) < order - first_row
    carried = jnp.where(live, total[...], 0.0).astype(BF16)
    green = (
        lax.dot_general(
            left[...], carried, (((0,), (0,)), ((), ())), preferred_element_type=F32
        )
        * scale
    )
    exact_ref[...] = green
    sent_ref[...] = green.astype(BF16)


def partial_green(order, vertex, right, left):
    height, breadth = vertex.shape
    states = right.shape[1]
    depth = breadth // CHUNKS
    hbm = pl.BlockSpec(memory_space=pltpu.HBM)
    vmem = pl.BlockSpec(memory_space=pltpu.VMEM)
    return pl.pallas_call(
        functools.partial(partial_kernel, 1.0 / math.sqrt(breadth)),
        in_specs=[pl.BlockSpec(memory_space=pltpu.SMEM), hbm, hbm, hbm],
        out_specs=[vmem] * 2,
        out_shape=[
            jax.ShapeDtypeStruct((states, states), F32),
            jax.ShapeDtypeStruct((states, states), BF16),
        ],
        scratch_shapes=[
            pltpu.VMEM((CHUNKS, height, depth), BF16),
            pltpu.VMEM((CHUNKS, depth, states), BF16),
            pltpu.VMEM((height, states), BF16),
            pltpu.VMEM((height, states), F32),
            pltpu.SemaphoreType.DMA((2 * CHUNKS + 1,)),
        ],
        compiler_params=pltpu.CompilerParams(vmem_limit_bytes=24 * MIB),
        cost_estimate=pl.CostEstimate(
            flops=2 * height * states * (breadth + states),
            bytes_accessed=2 * (height * breadth + breadth * states + height * states),
            transcendentals=0,
        ),
        name="partial_green",
    )(order, *[pltpu.with_memory_space_constraint(x, pltpu.HBM) for x in (vertex, right, left)])


def green_kernel(exact_ref, got_ref, green_ref):
    green_ref[...] = (exact_ref[...] + got_ref[...].astype(F32)).astype(BF16)


def whole_green(exact, got):
    vmem = pl.BlockSpec(memory_space=pltpu.VMEM)
    return pl.pallas_call(
        green_kernel,
        in_specs=[vmem] * 2,
        out_specs=vmem,
        out_shape=jax.ShapeDtypeStruct(exact.shape, BF16),
        compiler_params=pltpu.CompilerParams(vmem_limit_bytes=16 * MIB),
        cost_estimate=pl.CostEstimate(
            flops=exact.size, bytes_accessed=8 * exact.size, transcendentals=0
        ),
        name="whole_green",
    )(exact, got)


def fold_walker(green, pick_mom, pick_freq, tile_sum):
    rows, width = pick_mom.shape[0], pick_freq.shape[0]
    picked = jnp.dot(
        jnp.concatenate([pick_mom, pick_freq], axis=0), green, preferred_element_type=F32
    )
    by_mom = split_rows(picked[:rows])
    both = jnp.dot(by_mom, tile_sum, preferred_element_type=F32)
    folded = split_rows(both[:rows] + both[rows:])
    by_freq = split_rows(picked[rows:])
    terms = across(folded, by_freq)
    terms = terms[:rows] + terms[rows:]
    return terms[:, :width] + terms[:, width:]


def picks(mom_ref, freq_ref, rows, width):
    states = mom_ref.shape[1]
    per_row = rows // NMOM
    mom = lax.broadcasted_iota(jnp.int32, (rows, states), 0) // per_row == mom_ref[...]
    freq = lax.broadcasted_iota(jnp.int32, (width, states), 0) == freq_ref[...]
    return mom.astype(F32).astype(BF16), freq.astype(F32).astype(BF16)


def own_kernel(green_ref, sums_ref, mom_ref, freq_ref, out_ref):
    pick_mom, pick_freq = picks(mom_ref, freq_ref, *out_ref.shape)
    out_ref[...] = fold_walker(green_ref[...], pick_mom, pick_freq, sums_ref[1])


def sigma_kernel(factor, cells_ref, below_ref, above_ref, sums_ref, mom_ref, freq_ref, out_ref, last_ref):
    pick_mom, pick_freq = picks(mom_ref, freq_ref, *cells_ref.shape)
    upper = lax.axis_index("blk") % 2
    cells = (
        cells_ref[...]
        + fold_walker(below_ref[...], pick_mom, pick_freq, sums_ref[upper])
        + fold_walker(above_ref[...], pick_mom, pick_freq, sums_ref[1 - upper])
    ) * factor
    rows, width = out_ref.shape
    owner = lax.broadcasted_iota(jnp.int32, (rows, width), 0) * lax.axis_size(
        "pair"
    ) + lax.axis_index("pair")
    fold = NFREQ // width
    result = jnp.zeros((rows, width), F32)
    for part in range(fold):
        result = jnp.where(
            owner % fold == part, cells[:, part * width : (part + 1) * width], result
        )
    out_ref[...] = result

    @pl.when(upper == 1)
    def _():
        last_ref[...] = below_ref[...]

    @pl.when(upper == 0)
    def _():
        last_ref[...] = above_ref[...]


def small_call(kernel, shape, flops, name):
    vmem = pl.BlockSpec(memory_space=pltpu.VMEM)

    def call(*operands):
        return pl.pallas_call(
            kernel,
            in_specs=[vmem] * len(operands),
            out_specs=jax.tree.map(lambda _: vmem, shape),
            out_shape=shape,
            compiler_params=pltpu.CompilerParams(vmem_limit_bytes=16 * MIB),
            cost_estimate=pl.CostEstimate(
                flops=flops, bytes_accessed=sum(2 * x.size for x in operands), transcendentals=0
            ),
            name=name,
        )(*operands)

    return call


def chi_kernel(walkers, scale, *refs):
    greens, tile_ref, rest = refs[:walkers], refs[walkers], refs[walkers + 1 :]
    out_ref = rest[-1]
    half = out_ref.shape[1]
    first = pl.multiple_of(lax.axis_index("pair") * half, half)
    tile = tile_ref[0]
    total = None if len(rest) == 1 else rest[0][0]
    for green in greens:
        upper = green[pl.ds(first, half), :]
        inner = jnp.dot(upper, tile, preferred_element_type=F32).astype(BF16)
        term = lax.dot_general(
            inner, green[...], (((1,), (1,)), ((), ())), preferred_element_type=F32
        )
        total = term if total is None else total + term
    out_ref[0] = (total * scale).astype(out_ref.dtype)


def chi_terms(greens, tiles, running, scale, dtype, limit):
    count, states, _ = tiles.shape
    half = states // 2
    extra = [] if running is None else [running]
    whole = pl.BlockSpec((states, states), lambda t: (0, 0))
    rows = pl.BlockSpec((1, half, states), lambda t: (t, 0, 0))
    return pl.pallas_call(
        functools.partial(chi_kernel, len(greens), scale),
        grid=(count,),
        in_specs=[whole] * len(greens)
        + [pl.BlockSpec((1, states, states), lambda t: (t, 0, 0))]
        + [rows] * len(extra),
        out_specs=rows,
        out_shape=jax.ShapeDtypeStruct((count, half, states), dtype),
        compiler_params=pltpu.CompilerParams(vmem_limit_bytes=limit * MIB),
        cost_estimate=pl.CostEstimate(
            flops=len(greens) * count * 4 * half * states * states,
            bytes_accessed=2 * states * states * (count + len(greens)) + 4 * count * half * states,
            transcendentals=0,
        ),
        name="chi_terms",
    )(*greens, tiles, *[pltpu.with_memory_space_constraint(x, pltpu.HBM) for x in extra])


def moves(mesh_shape):
    blk, pair = mesh_shape

    def flat(rule):
        return [(b * pair + p, rule(b, p)) for b in range(blk) for p in range(pair)]

    other = flat(lambda b, p: b * pair + (p + 1) % pair)
    core = flat(lambda b, p: (b ^ 1) * pair + p)

    def along(even, odd):
        return flat(lambda b, p: ((b + (odd if b % 2 else even)) % blk) * pair + p)

    return other, core, along(2, 2), along(-2, -2)


def send(value, pairs):
    return lax.ppermute(value, BOTH, pairs)


def per_device(vertex, left_phase, right_phase, tiles, orders, momentum, frequency):
    states = right_phase.shape[2]
    half = states // 2
    blk, pair = lax.axis_size("blk"), lax.axis_size("pair")
    other, core, upward, downward = moves((blk, pair))

    with jax.named_scope("green"):
        exact, sent = partial_green(orders, vertex[0], right_phase[0], left_phase[0])
        received = send(sent, other)
        green = whole_green(exact, received)

    with jax.named_scope("tile_sums"):
        green, later_tiles = lax.optimization_barrier((green, tiles))
        own_sum = jnp.sum(later_tiles.astype(F32), axis=0)
        own_short = own_sum.astype(BF16)
        chip_sum = (own_sum + send(own_short, core).astype(F32)).astype(BF16)
        sums = jnp.stack([own_short, chip_sum])

    with jax.named_scope("window"):
        mom, freq = momentum[None, :], frequency[None, :]
        green_core = send(green, core)
        below = send(green, upward)
        above = send(green, downward)
        running = chi_terms([green, green_core], tiles, None, 1.0, F32, 24)
        cells = small_call(
            own_kernel, jax.ShapeDtypeStruct((blk, NFREQ), F32), 200_000_000, "own_cells"
        )(green, sums, mom, freq)
        running, cells, below, above = lax.optimization_barrier((running, cells, below, above))

    with jax.named_scope("sigma"):
        factor = 1.0 / math.sqrt(
            5.0 * tiles.shape[0] * blk * states * states / (NMOM * NFREQ)
        ) / math.sqrt(states)
        cells, last = small_call(
            functools.partial(sigma_kernel, factor),
            [
                jax.ShapeDtypeStruct((blk, NMOM * NFREQ // (blk * pair)), F32),
                jax.ShapeDtypeStruct(green.shape, BF16),
            ],
            400_000_000,
            "sigma_cells",
        )(cells, below, above, sums, mom, freq)
        running, cells, last = lax.optimization_barrier((running, cells, last))
        green_last = send(last, core)
        spread = lax.all_to_all(cells, "blk", 0, 0, tiled=True)

    with jax.named_scope("chi"):
        far = [below, above, green_last]
        suscept = chi_terms(far, tiles, running, 1.0 / math.sqrt(states), BF16, 24)
        suscept, spread = lax.optimization_barrier((suscept, spread))
        owned = jnp.sum(spread, axis=0)
    return suscept, owned


def solution(mesh):
    in_specs = (
        P("blk", "pair", None),
        P("blk", "pair", None),
        P("blk", None, None),
        P("blk", None, None),
        P("blk"),
        P(),
        P(),
    )
    out_specs = (P("blk", "pair", None), P(("blk", "pair")))
    return jax.shard_map(
        per_device, mesh=mesh, in_specs=in_specs, out_specs=out_specs, check_vma=False
    )
```

```python
import functools
import math

import jax
import jax.numpy as jnp
from jax import lax
from jax.experimental import pallas as pl
from jax.experimental.pallas import tpu as pltpu
from jax.sharding import PartitionSpec as P

NMOM = 64
NFREQ = 32
BOTH = ("blk", "pair")
F32 = jnp.float32
BF16 = jnp.bfloat16
CHUNKS = 8
MIB = 1024 * 1024


def split_rows(value):
    high = value.astype(BF16)
    return jnp.concatenate([high, (value - high.astype(F32)).astype(BF16)], axis=0)


def across(left, right):
    return lax.dot_general(left, right, (((1,), (1,)), ((), ())), preferred_element_type=F32)


def partial_kernel(
    scale, order_ref, vertex_hbm, right_hbm, left_hbm, exact_ref, sent_ref,
    vertex, right, left, total, sems,
):
    order = order_ref[0]
    first_row = lax.axis_index("pair") * total.shape[0]
    depth, states = right.shape[1:]
    copies = []
    for k in range(CHUNKS):
        span = pl.ds(k * depth, depth)
        copies.append(
            (
                pltpu.make_async_copy(right_hbm.at[span, :], right.at[k], sems.at[2 * k]),
                pltpu.make_async_copy(vertex_hbm.at[:, span], vertex.at[k], sems.at[2 * k + 1]),
            )
        )
    left_copy = pltpu.make_async_copy(left_hbm, left, sems.at[2 * CHUNKS])
    for pieces in copies:
        for copy in pieces:
            copy.start()
    left_copy.start()
    for k, pieces in enumerate(copies):
        for copy in pieces:
            copy.wait()

        @pl.when(order < (k + 1) * depth)
        def _():
            rows = lax.broadcasted_iota(jnp.int32, (depth, states), 0)
            right[k] = jnp.where(rows < order - k * depth, right[k], jnp.zeros_like(right[k]))

        product = jnp.dot(vertex[k], right[k], preferred_element_type=F32)
        if k == 0:
            total[...] = product
        else:
            total[...] += product
    left_copy.wait()
    live = lax.broadcasted_iota(jnp.int32, total.shape, 0) < order - first_row
    carried = jnp.where(live, total[...], 0.0).astype(BF16)
    green = (
        lax.dot_general(
            left[...], carried, (((0,), (0,)), ((), ())), preferred_element_type=F32
        )
        * scale
    )
    exact_ref[...] = green
    sent_ref[...] = green.astype(BF16)


def partial_green(order, vertex, right, left):
    height, breadth = vertex.shape
    states = right.shape[1]
    depth = breadth // CHUNKS
    hbm = pl.BlockSpec(memory_space=pltpu.HBM)
    vmem = pl.BlockSpec(memory_space=pltpu.VMEM)
    return pl.pallas_call(
        functools.partial(partial_kernel, 1.0 / math.sqrt(breadth)),
        in_specs=[pl.BlockSpec(memory_space=pltpu.SMEM), hbm, hbm, hbm],
        out_specs=[vmem] * 2,
        out_shape=[
            jax.ShapeDtypeStruct((states, states), F32),
            jax.ShapeDtypeStruct((states, states), BF16),
        ],
        scratch_shapes=[
            pltpu.VMEM((CHUNKS, height, depth), BF16),
            pltpu.VMEM((CHUNKS, depth, states), BF16),
            pltpu.VMEM((height, states), BF16),
            pltpu.VMEM((height, states), F32),
            pltpu.SemaphoreType.DMA((2 * CHUNKS + 1,)),
        ],
        compiler_params=pltpu.CompilerParams(vmem_limit_bytes=24 * MIB),
        cost_estimate=pl.CostEstimate(
            flops=2 * height * states * (breadth + states),
            bytes_accessed=2 * (height * breadth + breadth * states + height * states),
            transcendentals=0,
        ),
        name="partial_green",
    )(order, *[pltpu.with_memory_space_constraint(x, pltpu.HBM) for x in (vertex, right, left)])


def green_kernel(exact_ref, got_ref, green_ref):
    green_ref[...] = (exact_ref[...] + got_ref[...].astype(F32)).astype(BF16)


def whole_green(exact, got):
    vmem = pl.BlockSpec(memory_space=pltpu.VMEM)
    return pl.pallas_call(
        green_kernel,
        in_specs=[vmem] * 2,
        out_specs=vmem,
        out_shape=jax.ShapeDtypeStruct(exact.shape, BF16),
        compiler_params=pltpu.CompilerParams(vmem_limit_bytes=16 * MIB),
        cost_estimate=pl.CostEstimate(
            flops=exact.size, bytes_accessed=8 * exact.size, transcendentals=0
        ),
        name="whole_green",
    )(exact, got)


def fold_walker(green, pick_mom, pick_freq, tile_sum):
    rows, width = pick_mom.shape[0], pick_freq.shape[0]
    picked = jnp.dot(
        jnp.concatenate([pick_mom, pick_freq], axis=0), green, preferred_element_type=F32
    )
    by_mom = split_rows(picked[:rows])
    both = jnp.dot(by_mom, tile_sum, preferred_element_type=F32)
    folded = split_rows(both[:rows] + both[rows:])
    by_freq = split_rows(picked[rows:])
    terms = across(folded, by_freq)
    terms = terms[:rows] + terms[rows:]
    return terms[:, :width] + terms[:, width:]


def picks(mom_ref, freq_ref, rows, width):
    states = mom_ref.shape[1]
    per_row = rows // NMOM
    mom = lax.broadcasted_iota(jnp.int32, (rows, states), 0) // per_row == mom_ref[...]
    freq = lax.broadcasted_iota(jnp.int32, (width, states), 0) == freq_ref[...]
    return mom.astype(F32).astype(BF16), freq.astype(F32).astype(BF16)


def own_kernel(green_ref, sums_ref, mom_ref, freq_ref, out_ref):
    pick_mom, pick_freq = picks(mom_ref, freq_ref, *out_ref.shape)
    out_ref[...] = fold_walker(green_ref[...], pick_mom, pick_freq, sums_ref[1])


def sigma_kernel(factor, cells_ref, below_ref, above_ref, sums_ref, mom_ref, freq_ref, out_ref, last_ref):
    pick_mom, pick_freq = picks(mom_ref, freq_ref, *cells_ref.shape)
    upper = lax.axis_index("blk") % 2
    cells = (
        cells_ref[...]
        + fold_walker(below_ref[...], pick_mom, pick_freq, sums_ref[upper])
        + fold_walker(above_ref[...], pick_mom, pick_freq, sums_ref[1 - upper])
    ) * factor
    rows, width = out_ref.shape
    owner = lax.broadcasted_iota(jnp.int32, (rows, width), 0) * lax.axis_size(
        "pair"
    ) + lax.axis_index("pair")
    fold = NFREQ // width
    result = jnp.zeros((rows, width), F32)
    for part in range(fold):
        result = jnp.where(
            owner % fold == part, cells[:, part * width : (part + 1) * width], result
        )
    out_ref[...] = result

    @pl.when(upper == 1)
    def _():
        last_ref[...] = below_ref[...]

    @pl.when(upper == 0)
    def _():
        last_ref[...] = above_ref[...]


def small_call(kernel, shape, flops, name):
    vmem = pl.BlockSpec(memory_space=pltpu.VMEM)

    def call(*operands):
        return pl.pallas_call(
            kernel,
            in_specs=[vmem] * len(operands),
            out_specs=jax.tree.map(lambda _: vmem, shape),
            out_shape=shape,
            compiler_params=pltpu.CompilerParams(vmem_limit_bytes=16 * MIB),
            cost_estimate=pl.CostEstimate(
                flops=flops, bytes_accessed=sum(2 * x.size for x in operands), transcendentals=0
            ),
            name=name,
        )(*operands)

    return call


def chi_kernel(walkers, scale, *refs):
    greens, tile_ref, rest = refs[:walkers], refs[walkers], refs[walkers + 1 :]
    out_ref = rest[-1]
    half = out_ref.shape[1]
    first = pl.multiple_of(lax.axis_index("pair") * half, half)
    tile = tile_ref[0]
    total = None if len(rest) == 1 else rest[0][0]
    for green in greens:
        upper = green[pl.ds(first, half), :]
        inner = jnp.dot(upper, tile, preferred_element_type=F32).astype(BF16)
        term = lax.dot_general(
            inner, green[...], (((1,), (1,)), ((), ())), preferred_element_type=F32
        )
        total = term if total is None else total + term
    out_ref[0] = (total * scale).astype(out_ref.dtype)


def chi_terms(greens, tiles, running, scale, dtype, limit):
    count, states, _ = tiles.shape
    half = states // 2
    extra = [] if running is None else [running]
    whole = pl.BlockSpec((states, states), lambda t: (0, 0))
    rows = pl.BlockSpec((1, half, states), lambda t: (t, 0, 0))
    return pl.pallas_call(
        functools.partial(chi_kernel, len(greens), scale),
        grid=(count,),
        in_specs=[whole] * len(greens)
        + [pl.BlockSpec((1, states, states), lambda t: (t, 0, 0))]
        + [rows] * len(extra),
        out_specs=rows,
        out_shape=jax.ShapeDtypeStruct((count, half, states), dtype),
        compiler_params=pltpu.CompilerParams(vmem_limit_bytes=limit * MIB),
        cost_estimate=pl.CostEstimate(
            flops=len(greens) * count * 4 * half * states * states,
            bytes_accessed=2 * states * states * (count + len(greens)) + 4 * count * half * states,
            transcendentals=0,
        ),
        name="chi_terms",
    )(*greens, tiles, *[pltpu.with_memory_space_constraint(x, pltpu.HBM) for x in extra])


def moves(mesh_shape):
    blk, pair = mesh_shape

    def flat(rule):
        return [(b * pair + p, rule(b, p)) for b in range(blk) for p in range(pair)]

    other = flat(lambda b, p: b * pair + (p + 1) % pair)
    core = flat(lambda b, p: (b ^ 1) * pair + p)

    def along(even, odd):
        return flat(lambda b, p: ((b + (odd if b % 2 else even)) % blk) * pair + p)

    return other, core, along(2, 2), along(-2, -2)


def send(value, pairs):
    return lax.ppermute(value, BOTH, pairs)


def per_device(vertex, left_phase, right_phase, tiles, orders, momentum, frequency):
    states = right_phase.shape[2]
    half = states // 2
    blk, pair = lax.axis_size("blk"), lax.axis_size("pair")
    other, core, upward, downward = moves((blk, pair))

    with jax.named_scope("green"):
        exact, sent = partial_green(orders, vertex[0], right_phase[0], left_phase[0])
        received = send(sent, other)
        green = whole_green(exact, received)

    with jax.named_scope("tile_sums"):
        green, later_tiles = lax.optimization_barrier((green, tiles))
        own_sum = jnp.sum(later_tiles.astype(F32), axis=0)
        own_short = own_sum.astype(BF16)
        chip_sum = (own_sum + send(own_short, core).astype(F32)).astype(BF16)
        sums = jnp.stack([own_short, chip_sum])

    with jax.named_scope("window"):
        mom, freq = momentum[None, :], frequency[None, :]
        green_core = send(green, core)
        below = send(green, upward)
        above = send(green, downward)
        running = chi_terms([green, green_core], tiles, None, 1.0, F32, 24)
        cells = small_call(
            own_kernel, jax.ShapeDtypeStruct((blk, NFREQ), F32), 200_000_000, "own_cells"
        )(green, sums, mom, freq)
        running, cells, below, above = lax.optimization_barrier((running, cells, below, above))

    with jax.named_scope("sigma"):
        factor = 1.0 / math.sqrt(
            5.0 * tiles.shape[0] * blk * states * states / (NMOM * NFREQ)
        ) / math.sqrt(states)
        cells, last = small_call(
            functools.partial(sigma_kernel, factor),
            [
                jax.ShapeDtypeStruct((blk, NMOM * NFREQ // (blk * pair)), F32),
                jax.ShapeDtypeStruct(green.shape, BF16),
            ],
            400_000_000,
            "sigma_cells",
        )(cells, below, above, sums, mom, freq)
        running, cells, last = lax.optimization_barrier((running, cells, last))
        green_last = send(last, core)
        spread = lax.all_to_all(cells, "blk", 0, 0, tiled=True)

    with jax.named_scope("chi"):
        far = [below, above, green_last]
        suscept = chi_terms(far, tiles, running, 1.0 / math.sqrt(states), BF16, 24)
        suscept, spread = lax.optimization_barrier((suscept, spread))
        owned = jnp.sum(spread, axis=0)
    return suscept, owned


def solution(mesh):
    in_specs = (
        P("blk", "pair", None),
        P("blk", "pair", None),
        P("blk", None, None),
        P("blk", None, None),
        P("blk"),
        P(),
        P(),
    )
    out_specs = (P("blk", "pair", None), P(("blk", "pair")))
    return jax.shard_map(
        per_device, mesh=mesh, in_specs=in_specs, out_specs=out_specs, check_vma=False
    )
```
